32 devices in a mesh: expert: 8 (over y, x, core), tensor: 4 (over z).
Axes of the slice: x: 2, y: 2, z: 4, core: 2. Of those that a mesh axis runs over, the one named last changes fastest.
Arguments:
- tokens: bfloat16 [512, 4096], P('expert', 'tensor'), may hold values from -6 to 6
- expert_ids: int32 [512, 8], P('expert'), may hold values from 0 to 7, all different within a row; in each aligned block of 64 rows (0 to 63, 64 to 127, ...) at most 64 rows name the same one
- gate_weights: float32 [512, 8], P('expert'), may hold values from 0.1 to 1
- w_gate: bfloat16 [8, 4096, 1536], P('expert', None, 'tensor'), may hold values from -0.09375 to 0.09375
- w_up: bfloat16 [8, 4096, 1536], P('expert', None, 'tensor'), may hold values from -0.09375 to 0.09375
- w_down: bfloat16 [8, 1536, 4096], P('expert', 'tensor'), may hold values from -0.15625 to 0.15625
Outputs:
- mixed: bfloat16 [512, 4096], P('expert', 'tensor')
The draws below stay inside these ranges and needn't reach their ends.
Inputs may be any that keep to these rules, and one draw needn't show every extreme that they name: `expert_ids`: each row names 8 different experts. Within each aligned block of 64 rows no expert is named by more than 64 rows, and in every draw some expert is named by exactly 64 rows of some block.
All inputs are finite; a program needn't handle non-finite values.
Results may differ from the reference program's by a relative error of at most 0.02.
Values may be sent and summed in bfloat16 or wider, within the bound.
No kernel may reach another device: no remote copies, remote signals or barrier semaphores. Data moves between devices by JAX's collectives and lax.ppermute only.
A program may use at most 64 MiB of HBM per device.

```python
import math
import jax
import jax.numpy as jnp
import numpy as np
from jax import lax

D = 4096
FF = 1536
TOP = 8
TOK_DEV = 64
EXPERTS = 8
CAP = 64
TOKENS = 512
N_EXPERT = 8
N_TENSOR = 4


def level_of(rng, shape, shards, low, high):
    gain, own = 1.0, jax.random.fold_in(rng, 6)
    for dim, shards_of in shards:
        draws = jnp.exp(jax.random.uniform(jax.random.fold_in(own, dim), (shards_of,), jnp.float32, low / len(shards), high / len(shards)))
        gain = gain * jnp.repeat(draws, shape[dim] // shards_of).reshape([-1 if axis == dim else 1 for axis in range(len(shape))])
    return gain


def shared_out(rng, own, number, rows, count, top, reach, skew):
    order = jax.random.permutation(rng, count)
    heavy_load, common = load_shares(count, rows * top, reach, skew, True), load_shares(count, rows * top, reach, skew, False)
    places = jnp.arange(count)

    def named(tallies, offset_by):
        used = int((tallies > 0).sum())
        fixed = max(1, used // 4)
        shifted = fixed + (places - fixed + offset_by * (used - fixed)) % max(1, count - fixed)
        return jnp.zeros((count,), jnp.int32).at[order[jnp.where(places < fixed, places, shifted)]].set(jnp.asarray(tallies, jnp.int32))

    tallies = jnp.where(number % 4 == 0, named(heavy_load, number // 4), named(common, number - number // 4 - 1))
    mixed = jax.random.permutation(jax.random.fold_in(own, 3), count)
    giver, sink = mixed[0:count // 2 * 2:2], mixed[1:count // 2 * 2:2]
    margin = jnp.minimum(tallies[giver] - 1, reach - tallies[sink]) // 2
    margin = jnp.where((giver == order[0]) | (sink == order[0]) | (tallies[sink] == 0), 0, jnp.maximum(margin, 0))
    shifted = jax.random.randint(jax.random.fold_in(own, 4), (count // 2,), 0, 1 << 20) % (margin + 1)
    tallies = tallies.at[giver].add(-shifted).at[sink].add(shifted)
    labels = jnp.searchsorted(jnp.cumsum(tallies), jnp.arange(rows * top), side="right").astype(jnp.int32)
    listing = labels.reshape(top, rows).T
    listing = listing[jax.random.permutation(jax.random.fold_in(own, 1), rows)]
    offset_by = jax.random.randint(jax.random.fold_in(own, 2), (rows, 1), 0, top)
    return jnp.take_along_axis(listing, (jnp.arange(top)[None, :] + offset_by) % top, axis=1)


def load_shares(amount, total, reach, skew, full):
    portions = [(1 << 20) // math.isqrt(grade ** skew) + 1 for grade in range(1, amount + 1)]
    largest = reach if full else min(reach, max(-(-total // amount), total * portions[0] // sum(portions)))
    least = 1 if total - largest >= amount - 1 else 0
    counts, rest = [largest] + [least] * (amount - 1), total - largest - least * (amount - 1)
    while rest > 0:
        free = [i for i in range(1, amount) if counts[i] < largest] or [i for i in range(1, amount) if counts[i] < reach]
        pool, remaining = sum([portions[i] for i in free]), rest
        for i in free:
            extra = min(reach - counts[i], max(1, remaining * portions[i] // pool), rest)
            counts[i] = counts[i] + extra
            rest = rest - extra
    return np.array(counts)


def bell_draw(own_key, shape, scale, bound, shards=(), held_as=jnp.bfloat16):
    array = jax.random.normal(own_key, shape, jnp.float32) * scale
    if len(shards) > 0:
        array = level_of(own_key, shape, shards, -0.22, 0.18) * array
    return jnp.clip(array, min=-bound, max=bound).astype(held_as)


def setup_inputs(seed: int = 0) -> dict:
    key_of = jax.random.split(jax.random.key(seed), 7)
    tokens = bell_draw(key_of[0], (TOKENS, D), 1.0, 6.0, ((0, 8), (1, 4)))
    expert_ids_keys = jax.random.split(jax.random.fold_in(key_of[1], 1), TOKENS // TOK_DEV)
    expert_ids_turns = jax.random.permutation(jax.random.fold_in(key_of[1], 3), TOKENS // TOK_DEV)
    expert_ids = jax.vmap(lambda own, number: shared_out(jax.random.fold_in(key_of[1], 2), own, number, TOK_DEV, EXPERTS, TOP, CAP, 2))(expert_ids_keys, expert_ids_turns).reshape((TOKENS, TOP))
    gate_weights = jnp.clip(0.1 + 0.9 * jax.random.uniform(key_of[2], (TOKENS, TOP), jnp.float32) ** level_of(key_of[2], (TOKENS, TOP), ((0, 8),), -0.2, 0.2), 0.1, 1.0)
    w_gate = bell_draw(key_of[3], (EXPERTS, D, FF), D ** -0.5, 0.09375, ((0, 8), (2, 4)))
    w_up = bell_draw(key_of[4], (EXPERTS, D, FF), D ** -0.5, 0.09375, ((0, 8), (2, 4)))
    w_down = bell_draw(key_of[5], (EXPERTS, FF, D), FF ** -0.5, 0.15625, ((0, 8), (1, 4)))
    return dict(tokens=tokens, expert_ids=expert_ids, gate_weights=gate_weights, w_gate=w_gate, w_up=w_up, w_down=w_down)


def run_expert(operands):
    rows_in, gate_mat, up_mat, down_mat = operands
    gate = jnp.dot(rows_in, gate_mat, preferred_element_type=jnp.float32)
    up_val = jnp.dot(rows_in, up_mat, preferred_element_type=jnp.float32)
    hidden = (jax.nn.silu(gate) * up_val).astype(jnp.bfloat16)
    shard = FF // N_TENSOR
    hidden_blocks = hidden.reshape(hidden.shape[0], N_TENSOR, shard).astype(jnp.float32)
    down_blocks = down_mat.reshape(N_TENSOR, shard, D).astype(jnp.float32)
    partial_value = jnp.einsum("rsf,sfd->srd", hidden_blocks, down_blocks)
    rounded = lax.optimization_barrier(partial_value.astype(jnp.bfloat16))
    return jnp.sum(rounded.astype(jnp.float32), axis=0).astype(jnp.bfloat16)


def reference(tokens, expert_ids, gate_weights, w_gate, w_up, w_down):
    blocks = expert_ids.reshape(N_EXPERT, TOK_DEV * TOP)
    expert_range = jnp.arange(EXPERTS).astype(jnp.int32)
    onehot = (blocks[:, :, None] == expert_range[None, None, :]).astype(jnp.int32)
    slot_rank = jnp.sum((jnp.cumsum(onehot, axis=1) - onehot) * onehot, axis=2).astype(jnp.int32)
    block_index = jnp.arange(N_EXPERT).astype(jnp.int32)[:, None]
    slot_row = (block_index * CAP + slot_rank).astype(jnp.int32)
    flat_experts = blocks.reshape(-1)
    flat_rows = slot_row.reshape(-1)
    token_index = (jnp.arange(TOKENS * TOP) // TOP).astype(jnp.int32)
    dispatched = jnp.zeros((EXPERTS, N_EXPERT * CAP, D), jnp.bfloat16)
    dispatched = dispatched.at[flat_experts, flat_rows].set(tokens[token_index])
    expert_out = lax.map(run_expert, (dispatched, w_gate, w_up, w_down))
    picked = expert_out[flat_experts, flat_rows].reshape(TOKENS, TOP, D)
    mixed = jnp.sum(gate_weights[:, :, None] * picked.astype(jnp.float32), axis=1)
    return mixed.astype(jnp.bfloat16)
```

```python
import jax
import jax.numpy as jnp
from jax import lax
from jax.sharding import PartitionSpec as P


def slot_plan(tokens, expert_ids, gate_weights, w_gate, w_up, w_down):
    experts = lax.axis_size("expert")
    tok_rows, top_count = expert_ids.shape
    capacity = min(tok_rows, 3 * tok_rows * top_count // (2 * experts))
    slots_all = experts * capacity
    flat_ids = expert_ids.reshape(-1)
    onehot = (flat_ids[:, None] == jnp.arange(experts, dtype=jnp.int32)[None, :]).astype(jnp.int32)
    slot_rank = jnp.sum((jnp.cumsum(onehot, axis=0) - onehot) * onehot, axis=1)
    places = (flat_ids * capacity + slot_rank).reshape(tok_rows, top_count)
    slot_range = jnp.arange(slots_all, dtype=jnp.int32)[None, :]
    selector = jnp.zeros((tok_rows, slots_all), jnp.float32)
    combine_weights = jnp.zeros((tok_rows, slots_all), jnp.float32)
    for choice_index in range(top_count):
        hit = places[:, choice_index][:, None] == slot_range
        selector = selector + hit.astype(jnp.float32)
        combine_weights = combine_weights + jnp.where(
            hit, gate_weights[:, choice_index][:, None], 0.0
        )
    selector = selector.astype(jnp.bfloat16)
    outgoing = lax.dot_general(
        selector, tokens, (((0,), (0,)), ((), ())), preferred_element_type=jnp.float32
    ).astype(jnp.bfloat16)
    arrived = lax.all_to_all(outgoing, "expert", split_axis=0, concat_axis=0, tiled=True)
    hidden_units = w_gate.shape[2]
    paired = jnp.concatenate([w_gate[0], w_up[0]], axis=1)
    gate_up = jnp.dot(
        lax.all_gather(arrived, "tensor", axis=1, tiled=True),
        paired,
        preferred_element_type=jnp.float32,
    )
    hidden = (jax.nn.silu(gate_up[:, :hidden_units]) * gate_up[:, hidden_units:]).astype(
        jnp.bfloat16
    )
    summed = lax.psum_scatter(
        lax.dot_general(
            w_down[0], hidden, (((0,), (1,)), ((), ())), preferred_element_type=jnp.float32
        ).astype(jnp.bfloat16),
        "tensor",
        scatter_dimension=0,
        tiled=True,
    )
    returned = lax.all_to_all(summed, "expert", split_axis=1, concat_axis=1, tiled=True)
    mixed = lax.dot_general(
        combine_weights,
        returned.astype(jnp.float32),
        (((1,), (1,)), ((), ())),
        precision=lax.Precision.HIGHEST,
        preferred_element_type=jnp.float32,
    )
    return mixed.astype(jnp.bfloat16)


def toward(a, axis, flip):
    return lax.ppermute(a, axis, [(i, i ^ flip) for i in range(lax.axis_size(axis))])


def f32(a):
    return a.astype(jnp.float32)


def half(a):
    return a.astype(jnp.bfloat16)


def spread(a):
    mid = a.shape[0] // 2
    ax = toward(a, "expert", 2)
    ay = toward(a, "expert", 4)
    far_a = toward(ax[:mid], "expert", 4)
    far_b = toward(ay[mid:], "expert", 2)
    mine = jnp.concatenate([a, ax, ay, far_a, far_b], axis=0)
    other = toward(mine, "expert", 1)
    return mine, other


def collect(mine_of, other_of):
    got = toward(half(other_of()), "expert", 1)
    part = half(mine_of() + f32(got))
    rows = part.shape[0] // 4
    mid = rows // 2
    own, px, py, pd = (part[i * rows : (i + 1) * rows] for i in range(4))
    fx = toward(jnp.concatenate([px[:mid], pd[:mid]], axis=0), "expert", 2)
    fy = toward(jnp.concatenate([py[mid:], pd[mid:]], axis=0), "expert", 4)
    up = half(f32(py[:mid]) + f32(fx[mid:]))
    down = half(f32(px[mid:]) + f32(fy[mid:]))
    gy = toward(up, "expert", 4)
    gx = toward(down, "expert", 2)
    first = f32(own[:mid]) + f32(fx[:mid]) + f32(gy)
    second = f32(own[mid:]) + f32(fy[:mid]) + f32(gx)
    return jnp.concatenate([first, second], axis=0)


def gather_plan(tokens, expert_ids, gate_weights, w_gate, w_up, w_down):
    experts, shards = lax.axis_size("expert"), lax.axis_size("tensor")
    me, mz = lax.axis_index("expert"), lax.axis_index("tensor")
    _, cols = tokens.shape
    units = w_gate.shape[2]
    hits = expert_ids[:, :, None] == jnp.arange(experts, dtype=jnp.int32)
    table = jnp.sum(jnp.where(hits, gate_weights[:, :, None], 0.0), axis=1)
    terms, rest = [], table
    for _ in range(3):
        term = lax.reduce_precision(rest, 8, 7)
        terms.append(half(term))
        rest = rest - term
    terms = jnp.concatenate(terms, axis=1)
    terms = jnp.pad(terms, ((0, 0), (0, 128 - terms.shape[1])))

    zs = {k: toward(tokens, "tensor", k) for k in range(1, shards)}
    chunks = [[0], list(range(1, shards - 1)), [shards - 1]]
    acc = [0.0, 0.0]
    weight = None
    for n, ks in enumerate(chunks):
        parts = [tokens if k == 0 else zs[k] for k in ks]
        if n == 1:
            parts.append(terms)
        both = spread(jnp.concatenate(parts, axis=1) if len(parts) > 1 else parts[0])
        for i, k in enumerate(ks):
            at = (mz ^ k) * cols
            wk = jnp.concatenate(
                [lax.dynamic_slice_in_dim(w[0], at, cols, 0) for w in (w_gate, w_up)], axis=1
            )
            for h in range(2):
                acc[h] = acc[h] + jnp.dot(
                    both[h][:, i * cols : (i + 1) * cols], wk, preferred_element_type=jnp.float32
                )
        if n == 1:
            pick = jnp.arange(3 * experts, dtype=jnp.int32) % experts == me
            weight = [
                jnp.sum(jnp.where(pick, f32(b[:, len(ks) * cols :][:, : 3 * experts]), 0.0), axis=1)
                for b in both
            ]
    hidden = [
        half(jax.nn.silu(a[:, :units]) * a[:, units:] * w[:, None]) for a, w in zip(acc, weight)
    ]
    sums = {}
    for n, ks in reversed(list(enumerate(chunks))):
        wd = jnp.concatenate(
            [lax.dynamic_slice_in_dim(w_down[0], (mz ^ k) * cols, cols, 1) for k in ks], axis=1
        )
        total = collect(
            lambda: jnp.dot(hidden[0], wd, preferred_element_type=jnp.float32),
            lambda: jnp.dot(hidden[1], wd, preferred_element_type=jnp.float32),
        )
        for i, k in enumerate(ks):
            sums[k] = total[:, i * cols : (i + 1) * cols]
    mixed = sums[0]
    for k in range(1, shards):
        mixed = mixed + f32(toward(half(sums[k]), "tensor", k))
    return half(mixed)


def local(*args):
    tok_rows, top_count = args[1].shape
    experts, shards = lax.axis_size("expert"), lax.axis_size("tensor")
    capacity = min(tok_rows, 3 * tok_rows * top_count // (2 * experts))
    if capacity == tok_rows and experts == 1 << 3 and shards & (shards - 1) == 0 and shards > 2:
        return gather_plan(*args)
    return slot_plan(*args)


def solution(mesh):
    placed = (
        P("expert", "tensor"),
        P("expert", None),
        P("expert", None),
        P("expert", None, "tensor"),
        P("expert", None, "tensor"),
        P("expert", "tensor", None),
    )
    return jax.shard_map(
        local, mesh=mesh, in_specs=placed, out_specs=P("expert", "tensor"), check_vma=False
    )
```

```python
import jax
import jax.numpy as jnp
from jax import lax
from jax.experimental import pallas as pl
from jax.experimental.pallas import tpu as pltpu
from jax.sharding import PartitionSpec as P


IN_CHUNKS = [[0], [1], [2], [3]]
OUT_CHUNKS = [[3], [2], [1], [0]]
TERMS_IN = 2


def slot_plan(tokens, expert_ids, gate_weights, w_gate, w_up, w_down):
    experts = lax.axis_size("expert")
    tok_rows, top_count = expert_ids.shape
    capacity = min(tok_rows, 3 * tok_rows * top_count // (2 * experts))
    slots_all = experts * capacity
    flat_ids = expert_ids.reshape(-1)
    onehot = (flat_ids[:, None] == jnp.arange(experts, dtype=jnp.int32)[None, :]).astype(jnp.int32)
    slot_rank = jnp.sum((jnp.cumsum(onehot, axis=0) - onehot) * onehot, axis=1)
    places = (flat_ids * capacity + slot_rank).reshape(tok_rows, top_count)
    slot_range = jnp.arange(slots_all, dtype=jnp.int32)[None, :]
    selector = jnp.zeros((tok_rows, slots_all), jnp.float32)
    combine_weights = jnp.zeros((tok_rows, slots_all), jnp.float32)
    for choice_index in range(top_count):
        hit = places[:, choice_index][:, None] == slot_range
        selector = selector + hit.astype(jnp.float32)
        combine_weights = combine_weights + jnp.where(
            hit, gate_weights[:, choice_index][:, None], 0.0
        )
    selector = selector.astype(jnp.bfloat16)
    outgoing = lax.dot_general(
        selector, tokens, (((0,), (0,)), ((), ())), preferred_element_type=jnp.float32
    ).astype(jnp.bfloat16)
    arrived = lax.all_to_all(outgoing, "expert", split_axis=0, concat_axis=0, tiled=True)
    hidden_units = w_gate.shape[2]
    paired = jnp.concatenate([w_gate[0], w_up[0]], axis=1)
    gate_up = jnp.dot(
        lax.all_gather(arrived, "tensor", axis=1, tiled=True),
        paired,
        preferred_element_type=jnp.float32,
    )
    hidden = (jax.nn.silu(gate_up[:, :hidden_units]) * gate_up[:, hidden_units:]).astype(
        jnp.bfloat16
    )
    summed = lax.psum_scatter(
        lax.dot_general(
            w_down[0], hidden, (((0,), (1,)), ((), ())), preferred_element_type=jnp.float32
        ).astype(jnp.bfloat16),
        "tensor",
        scatter_dimension=0,
        tiled=True,
    )
    returned = lax.all_to_all(summed, "expert", split_axis=1, concat_axis=1, tiled=True)
    mixed = lax.dot_general(
        combine_weights,
        returned.astype(jnp.float32),
        (((1,), (1,)), ((), ())),
        precision=lax.Precision.HIGHEST,
        preferred_element_type=jnp.float32,
    )
    return mixed.astype(jnp.bfloat16)


def toward(a, move):
    experts, shards = lax.axis_size("expert"), lax.axis_size("tensor")
    pairs = []
    for e in range(experts):
        for z in range(shards):
            to_e, to_z = move(e, z)
            pairs.append((e * shards + z, to_e * shards + to_z))
    return lax.ppermute(a, ("expert", "tensor"), pairs)


def core_pair(a):
    return toward(a, lambda e, z: (e ^ 1, z))


def first_side(a):
    return toward(a, lambda e, z: (e ^ (2 << (e & 1)), z))


def second_side(a):
    return toward(a, lambda e, z: (e ^ (4 >> (e & 1)), z))


def along(a, k):
    return toward(a, lambda e, z: (e, z ^ k))


def f32(a):
    return a.astype(jnp.float32)


def half(a):
    return a.astype(jnp.bfloat16)


def load_slices(places, sources, dim, grant):
    shard = sources[0].shape[dim] // lax.axis_size("tensor")
    shape = list(sources[0].shape[1:])
    shape[dim - 1] = shard
    width, count = shape[1], places.shape[0]

    def kernel(places_ref, *refs):
        ins, outs, sem = refs[: len(sources)], refs[len(sources) : -1], refs[-1]
        copies = []
        for k in range(count):
            part = pl.ds(pl.multiple_of(places_ref[k] * shard, shard), shard)
            for n, ref in enumerate(ins):
                src = ref.at[0, part, :] if dim == 1 else ref.at[0, :, part]
                dst = outs[k].at[:, pl.ds(n * width, width)]
                copies.append(pltpu.make_async_copy(src, dst, sem.at[len(copies)]))
        for copy in copies:
            copy.start()
        for copy in copies:
            copy.wait()

    out = pltpu.VMEM((shape[0], width * len(sources)), sources[0].dtype)
    return pl.pallas_call(
        kernel,
        out_shape=[out] * count,
        in_specs=[pl.BlockSpec(memory_space=pltpu.SMEM)]
        + [pl.BlockSpec(memory_space=pl.ANY)] * len(sources),
        out_specs=[pl.BlockSpec(memory_space=pltpu.VMEM)] * count,
        scratch_shapes=[pltpu.SemaphoreType.DMA((count * len(sources),))],
        compiler_params=pltpu.CompilerParams(vmem_limit_bytes=grant),
    )(places, *[pltpu.with_memory_space_constraint(a, pltpu.HBM) for a in sources])


def spread(a):
    rows = a.shape[0]
    pair = core_pair(a)
    side = first_side(jnp.concatenate([a, pair], axis=0))
    far = second_side(side[:rows])
    brought = jnp.concatenate([side, far], axis=0)
    swapped = core_pair(brought)
    return jnp.concatenate([a, brought], axis=0), jnp.concatenate([pair, swapped], axis=0)


def collect(mine_of, other_of):
    got = core_pair(half(other_of()))
    part = half(mine_of() + f32(got))
    rows = part.shape[0] // 4
    far = second_side(part[3 * rows :])
    near = half(f32(part[rows : 2 * rows]) + f32(far))
    side = first_side(jnp.concatenate([near, part[2 * rows : 3 * rows]], axis=0))
    swapped = core_pair(side[rows:])
    return f32(part[:rows]) + f32(side[:rows]) + f32(swapped)


def gather_plan(tokens, expert_ids, gate_weights, w_gate, w_up, w_down):
    experts, shards = lax.axis_size("expert"), lax.axis_size("tensor")
    me, mz = lax.axis_index("expert"), lax.axis_index("tensor")
    cols = tokens.shape[1]
    units = w_gate.shape[2]
    hits = expert_ids[:, :, None] == jnp.arange(experts, dtype=jnp.int32)
    table = jnp.sum(jnp.where(hits, gate_weights[:, :, None], 0.0), axis=1)
    terms, rest = [], table
    for _ in range(3):
        term = lax.reduce_precision(rest, 8, 7)
        terms.append(half(term))
        rest = rest - term
    terms = jnp.concatenate(terms, axis=1)
    terms = jnp.pad(terms, ((0, 0), (0, 128 - terms.shape[1])))

    places = mz ^ jnp.arange(shards, dtype=jnp.int32)
    pairs = load_slices(places, [w_gate, w_up], 1, 2 << 20)
    downs = load_slices(places, [w_down], 2, 2 << 20)
    zs = {k: along(tokens, k) for k in range(1, shards)}
    acc = [0.0, 0.0]
    weight = None
    for n, ks in enumerate(IN_CHUNKS):
        parts = [tokens if k == 0 else zs[k] for k in ks]
        if n == TERMS_IN:
            parts.append(terms)
        both = spread(jnp.concatenate(parts, axis=1) if len(parts) > 1 else parts[0])
        for i, k in enumerate(ks):
            for h in range(2):
                acc[h] = acc[h] + jnp.dot(
                    both[h][:, i * cols : (i + 1) * cols],
                    pairs[k],
                    preferred_element_type=jnp.float32,
                )
        acc = list(lax.optimization_barrier(tuple(acc)))
        if n == TERMS_IN:
            pick = jnp.arange(3 * experts, dtype=jnp.int32) % experts == me
            weight = [
                jnp.sum(jnp.where(pick, f32(b[:, len(ks) * cols :][:, : 3 * experts]), 0.0), axis=1)
                for b in both
            ]
    hidden = [
        half(jax.nn.silu(a[:, :units]) * a[:, units:] * w[:, None]) for a, w in zip(acc, weight)
    ]
    sums = {}
    for ks in OUT_CHUNKS:
        def product(h):
            return jnp.concatenate(
                [jnp.dot(hidden[h], downs[k], preferred_element_type=jnp.float32) for k in ks],
                axis=1,
            )

        total = collect(lambda: product(0), lambda: product(1))
        for i, k in enumerate(ks):
            sums[k] = total[:, i * cols : (i + 1) * cols]
            if k:
                sums[k] = half(sums[k])
    mixed = sums[0]
    for k in range(1, shards):
        mixed = mixed + f32(along(sums[k], k))
    return half(mixed)


def local(*args):
    tok_rows, top_count = args[1].shape
    experts, shards = lax.axis_size("expert"), lax.axis_size("tensor")
    capacity = min(tok_rows, 3 * tok_rows * top_count // (2 * experts))
    if capacity == tok_rows and experts == 1 << 3 and shards & (shards - 1) == 0 and shards > 2:
        return gather_plan(*args)
    return slot_plan(*args)


def solution(mesh):
    placed = (
        P("expert", "tensor"),
        P("expert", None),
        P("expert", None),
        P("expert", None, "tensor"),
        P("expert", None, "tensor"),
        P("expert", "tensor", None),
    )
    return jax.shard_map(
        local, mesh=mesh, in_specs=placed, out_specs=P("expert", "tensor"), check_vma=False
    )
```

```python
import jax
import jax.numpy as jnp
from jax import lax
from jax.experimental import pallas as pl
from jax.experimental.pallas import tpu as pltpu
from jax.sharding import PartitionSpec as P


IN_CHUNKS = [[0], [1], [2], [3]]
OUT_CHUNKS = [[3], [2], [1], [0]]
TERMS_IN = 2
IN_DIRECT = (0, 1, 2, 3)
OUT_DIRECT = (0, 1, 2, 3)


def slot_plan(tokens, expert_ids, gate_weights, w_gate, w_up, w_down):
    experts = lax.axis_size("expert")
    tok_rows, top_count = expert_ids.shape
    capacity = min(tok_rows, 3 * tok_rows * top_count // (2 * experts))
    slots_all = experts * capacity
    flat_ids = expert_ids.reshape(-1)
    onehot = (flat_ids[:, None] == jnp.arange(experts, dtype=jnp.int32)[None, :]).astype(jnp.int32)
    slot_rank = jnp.sum((jnp.cumsum(onehot, axis=0) - onehot) * onehot, axis=1)
    places = (flat_ids * capacity + slot_rank).reshape(tok_rows, top_count)
    slot_range = jnp.arange(slots_all, dtype=jnp.int32)[None, :]
    selector = jnp.zeros((tok_rows, slots_all), jnp.float32)
    combine_weights = jnp.zeros((tok_rows, slots_all), jnp.float32)
    for choice_index in range(top_count):
        hit = places[:, choice_index][:, None] == slot_range
        selector = selector + hit.astype(jnp.float32)
        combine_weights = combine_weights + jnp.where(
            hit, gate_weights[:, choice_index][:, None], 0.0
        )
    selector = selector.astype(jnp.bfloat16)
    outgoing = lax.dot_general(
        selector, tokens, (((0,), (0,)), ((), ())), preferred_element_type=jnp.float32
    ).astype(jnp.bfloat16)
    arrived = lax.all_to_all(outgoing, "expert", split_axis=0, concat_axis=0, tiled=True)
    hidden_units = w_gate.shape[2]
    paired = jnp.concatenate([w_gate[0], w_up[0]], axis=1)
    gate_up = jnp.dot(
        lax.all_gather(arrived, "tensor", axis=1, tiled=True),
        paired,
        preferred_element_type=jnp.float32,
    )
    hidden = (jax.nn.silu(gate_up[:, :hidden_units]) * gate_up[:, hidden_units:]).astype(
        jnp.bfloat16
    )
    summed = lax.psum_scatter(
        lax.dot_general(
            w_down[0], hidden, (((0,), (1,)), ((), ())), preferred_element_type=jnp.float32
        ).astype(jnp.bfloat16),
        "tensor",
        scatter_dimension=0,
        tiled=True,
    )
    returned = lax.all_to_all(summed, "expert", split_axis=1, concat_axis=1, tiled=True)
    mixed = lax.dot_general(
        combine_weights,
        returned.astype(jnp.float32),
        (((1,), (1,)), ((), ())),
        precision=lax.Precision.HIGHEST,
        preferred_element_type=jnp.float32,
    )
    return mixed.astype(jnp.bfloat16)


def toward(a, move):
    experts, shards = lax.axis_size("expert"), lax.axis_size("tensor")
    pairs = []
    for e in range(experts):
        for z in range(shards):
            to_e, to_z = move(e, z)
            pairs.append((e * shards + z, to_e * shards + to_z))
    return lax.ppermute(a, ("expert", "tensor"), pairs)


def core_pair(a):
    return toward(a, lambda e, z: (e ^ 1, z))


def first_side(a):
    return toward(a, lambda e, z: (e ^ (2 << (e & 1)), z))


def second_side(a):
    return toward(a, lambda e, z: (e ^ (4 >> (e & 1)), z))


def corner(a):
    return toward(a, lambda e, z: (e ^ 6, z))


def along(a, k):
    return toward(a, lambda e, z: (e, z ^ k))


def f32(a):
    return a.astype(jnp.float32)


def half(a):
    return a.astype(jnp.bfloat16)


def load_slices(places, sources, dim, grant):
    shard = sources[0].shape[dim] // lax.axis_size("tensor")
    shape = list(sources[0].shape[1:])
    shape[dim - 1] = shard
    width, count = shape[1], places.shape[0]

    def kernel(places_ref, *refs):
        ins, outs, sem = refs[: len(sources)], refs[len(sources) : -1], refs[-1]
        copies = []
        for k in range(count):
            part = pl.ds(pl.multiple_of(places_ref[k] * shard, shard), shard)
            for n, ref in enumerate(ins):
                src = ref.at[0, part, :] if dim == 1 else ref.at[0, :, part]
                dst = outs[k].at[:, pl.ds(n * width, width)]
                copies.append(pltpu.make_async_copy(src, dst, sem.at[len(copies)]))
        for copy in copies:
            copy.start()
        for copy in copies:
            copy.wait()

    out = pltpu.VMEM((shape[0], width * len(sources)), sources[0].dtype)
    return pl.pallas_call(
        kernel,
        out_shape=[out] * count,
        in_specs=[pl.BlockSpec(memory_space=pltpu.SMEM)]
        + [pl.BlockSpec(memory_space=pl.ANY)] * len(sources),
        out_specs=[pl.BlockSpec(memory_space=pltpu.VMEM)] * count,
        scratch_shapes=[pltpu.SemaphoreType.DMA((count * len(sources),))],
        compiler_params=pltpu.CompilerParams(vmem_limit_bytes=grant),
    )(places, *[pltpu.with_memory_space_constraint(a, pltpu.HBM) for a in sources])


def spread(a, tag):
    rows = a.shape[0]
    pair = core_pair(a)
    side = first_side(jnp.concatenate([a, pair], axis=0))
    far = corner(a) if int(tag) in IN_DIRECT else second_side(side[:rows])
    brought = jnp.concatenate([side, far], axis=0)
    swapped = core_pair(brought)
    return jnp.concatenate([a, brought], axis=0), jnp.concatenate([pair, swapped], axis=0)


def collect(mine_of, other_of, tag):
    got = core_pair(half(other_of()))
    part = half(mine_of() + f32(got))
    rows = part.shape[0] // 4
    own = part[:rows]
    if int(tag) in OUT_DIRECT:
        far = corner(part[3 * rows :])
        side = first_side(part[rows : 3 * rows])
        swapped = core_pair(side[rows:])
        return f32(own) + f32(far) + f32(side[:rows]) + f32(swapped)
    far = second_side(part[3 * rows :])
    near = half(f32(part[rows : 2 * rows]) + f32(far))
    side = first_side(jnp.concatenate([near, part[2 * rows : 3 * rows]], axis=0))
    swapped = core_pair(side[rows:])
    return f32(own) + f32(side[:rows]) + f32(swapped)


def gather_plan(tokens, expert_ids, gate_weights, w_gate, w_up, w_down):
    experts, shards = lax.axis_size("expert"), lax.axis_size("tensor")
    me, mz = lax.axis_index("expert"), lax.axis_index("tensor")
    cols = tokens.shape[1]
    units = w_gate.shape[2]
    hits = expert_ids[:, :, None] == jnp.arange(experts, dtype=jnp.int32)
    table = jnp.sum(jnp.where(hits, gate_weights[:, :, None], 0.0), axis=1)
    terms, rest = [], table
    for _ in range(3):
        term = lax.reduce_precision(rest, 8, 7)
        terms.append(half(term))
        rest = rest - term
    terms = jnp.concatenate(terms, axis=1)
    terms = jnp.pad(terms, ((0, 0), (0, 128 - terms.shape[1])))

    places = mz ^ jnp.arange(shards, dtype=jnp.int32)
    pairs = load_slices(places, [w_gate, w_up], 1, 2 << 20)
    downs = load_slices(places, [w_down], 2, 2 << 20)
    zs = {k: along(tokens, k) for k in range(1, shards)}
    acc = [0.0, 0.0]
    weight = None
    for n, ks in enumerate(IN_CHUNKS):
        parts = [tokens if k == 0 else zs[k] for k in ks]
        if n == TERMS_IN:
            parts.append(terms)
        both = spread(jnp.concatenate(parts, axis=1) if len(parts) > 1 else parts[0], str(n))
        for i, k in enumerate(ks):
            for h in range(2):
                acc[h] = acc[h] + jnp.dot(
                    both[h][:, i * cols : (i + 1) * cols],
                    pairs[k],
                    preferred_element_type=jnp.float32,
                )
        acc = list(lax.optimization_barrier(tuple(acc)))
        if n == TERMS_IN:
            pick = jnp.arange(3 * experts, dtype=jnp.int32) % experts == me
            weight = [
                jnp.sum(jnp.where(pick, f32(b[:, len(ks) * cols :][:, : 3 * experts]), 0.0), axis=1)
                for b in both
            ]
    hidden = [
        half(jax.nn.silu(a[:, :units]) * a[:, units:] * w[:, None]) for a, w in zip(acc, weight)
    ]
    sums = {}
    for n, ks in enumerate(OUT_CHUNKS):
        def product(h):
            return jnp.concatenate(
                [jnp.dot(hidden[h], downs[k], preferred_element_type=jnp.float32) for k in ks],
                axis=1,
            )

        total = collect(lambda: product(0), lambda: product(1), str(n))
        for i, k in enumerate(ks):
            sums[k] = total[:, i * cols : (i + 1) * cols]
            if k:
                sums[k] = half(sums[k])
    mixed = sums[0]
    for k in range(1, shards):
        mixed = mixed + f32(along(sums[k], k))
    return half(mixed)


def local(*args):
    tok_rows, top_count = args[1].shape
    experts, shards = lax.axis_size("expert"), lax.axis_size("tensor")
    capacity = min(tok_rows, 3 * tok_rows * top_count // (2 * experts))
    if capacity == tok_rows and experts == 1 << 3 and shards & (shards - 1) == 0 and shards > 2:
        return gather_plan(*args)
    return slot_plan(*args)


def solution(mesh):
    placed = (
        P("expert", "tensor"),
        P("expert", None),
        P("expert", None),
        P("expert", None, "tensor"),
        P("expert", None, "tensor"),
        P("expert", "tensor", None),
    )
    return jax.shard_map(
        local, mesh=mesh, in_specs=placed, out_specs=P("expert", "tensor"), check_vma=False
    )
```

```python
import jax
import jax.numpy as jnp
from jax import lax
from jax.experimental import pallas as pl
from jax.experimental.pallas import tpu as pltpu
from jax.sharding import PartitionSpec as P


IN_CHUNKS = [[0], [1], [2], [3]]
OUT_CHUNKS = [[3], [2], [1], [0]]
TERMS_IN = 2
SPLIT = (3,)
IN_DIRECT = (0, 1, 2, 3)
OUT_DIRECT = (0, 1, 2, 3)


def slot_plan(tokens, expert_ids, gate_weights, w_gate, w_up, w_down):
    experts = lax.axis_size("expert")
    tok_rows, top_count = expert_ids.shape
    capacity = min(tok_rows, 3 * tok_rows * top_count // (2 * experts))
    slots_all = experts * capacity
    flat_ids = expert_ids.reshape(-1)
    onehot = (flat_ids[:, None] == jnp.arange(experts, dtype=jnp.int32)[None, :]).astype(jnp.int32)
    slot_rank = jnp.sum((jnp.cumsum(onehot, axis=0) - onehot) * onehot, axis=1)
    places = (flat_ids * capacity + slot_rank).reshape(tok_rows, top_count)
    slot_range = jnp.arange(slots_all, dtype=jnp.int32)[None, :]
    selector = jnp.zeros((tok_rows, slots_all), jnp.float32)
    combine_weights = jnp.zeros((tok_rows, slots_all), jnp.float32)
    for choice_index in range(top_count):
        hit = places[:, choice_index][:, None] == slot_range
        selector = selector + hit.astype(jnp.float32)
        combine_weights = combine_weights + jnp.where(
            hit, gate_weights[:, choice_index][:, None], 0.0
        )
    selector = selector.astype(jnp.bfloat16)
    outgoing = lax.dot_general(
        selector, tokens, (((0,), (0,)), ((), ())), preferred_element_type=jnp.float32
    ).astype(jnp.bfloat16)
    arrived = lax.all_to_all(outgoing, "expert", split_axis=0, concat_axis=0, tiled=True)
    hidden_units = w_gate.shape[2]
    paired = jnp.concatenate([w_gate[0], w_up[0]], axis=1)
    gate_up = jnp.dot(
        lax.all_gather(arrived, "tensor", axis=1, tiled=True),
        paired,
        preferred_element_type=jnp.float32,
    )
    hidden = (jax.nn.silu(gate_up[:, :hidden_units]) * gate_up[:, hidden_units:]).astype(
        jnp.bfloat16
    )
    summed = lax.psum_scatter(
        lax.dot_general(
            w_down[0], hidden, (((0,), (1,)), ((), ())), preferred_element_type=jnp.float32
        ).astype(jnp.bfloat16),
        "tensor",
        scatter_dimension=0,
        tiled=True,
    )
    returned = lax.all_to_all(summed, "expert", split_axis=1, concat_axis=1, tiled=True)
    mixed = lax.dot_general(
        combine_weights,
        returned.astype(jnp.float32),
        (((1,), (1,)), ((), ())),
        precision=lax.Precision.HIGHEST,
        preferred_element_type=jnp.float32,
    )
    return mixed.astype(jnp.bfloat16)


def toward(a, move):
    experts, shards = lax.axis_size("expert"), lax.axis_size("tensor")
    pairs = []
    for e in range(experts):
        for z in range(shards):
            to_e, to_z = move(e, z)
            pairs.append((e * shards + z, to_e * shards + to_z))
    return lax.ppermute(a, ("expert", "tensor"), pairs)


def core_pair(a):
    return toward(a, lambda e, z: (e ^ 1, z))


def first_side(a):
    return toward(a, lambda e, z: (e ^ (2 << (e & 1)), z))


def second_side(a):
    return toward(a, lambda e, z: (e ^ (4 >> (e & 1)), z))


def corner(a):
    return toward(a, lambda e, z: (e ^ 6, z))


def along(a, k):
    return toward(a, lambda e, z: (e, z ^ k))


def f32(a):
    return a.astype(jnp.float32)


def half(a):
    return a.astype(jnp.bfloat16)


def load_slices(places, sources, dim, grant):
    shard = sources[0].shape[dim] // lax.axis_size("tensor")
    shape = list(sources[0].shape[1:])
    shape[dim - 1] = shard
    width, count = shape[1], places.shape[0]

    def kernel(places_ref, *refs):
        ins, outs, sem = refs[: len(sources)], refs[len(sources) : -1], refs[-1]
        copies = []
        for k in range(count):
            part = pl.ds(pl.multiple_of(places_ref[k] * shard, shard), shard)
            for n, ref in enumerate(ins):
                src = ref.at[0, part, :] if dim == 1 else ref.at[0, :, part]
                dst = outs[k].at[:, pl.ds(n * width, width)]
                copies.append(pltpu.make_async_copy(src, dst, sem.at[len(copies)]))
        for copy in copies:
            copy.start()
        for copy in copies:
            copy.wait()

    out = pltpu.VMEM((shape[0], width * len(sources)), sources[0].dtype)
    return pl.pallas_call(
        kernel,
        out_shape=[out] * count,
        in_specs=[pl.BlockSpec(memory_space=pltpu.SMEM)]
        + [pl.BlockSpec(memory_space=pl.ANY)] * len(sources),
        out_specs=[pl.BlockSpec(memory_space=pltpu.VMEM)] * count,
        scratch_shapes=[pltpu.SemaphoreType.DMA((count * len(sources),))],
        compiler_params=pltpu.CompilerParams(vmem_limit_bytes=grant),
    )(places, *[pltpu.with_memory_space_constraint(a, pltpu.HBM) for a in sources])


def spread(a, tag):
    rows = a.shape[0]
    pair = core_pair(a)
    side = first_side(jnp.concatenate([a, pair], axis=0))
    far = corner(a) if int(tag) in IN_DIRECT else second_side(side[:rows])
    brought = jnp.concatenate([side, far], axis=0)
    swapped = core_pair(brought)
    return jnp.concatenate([a, brought], axis=0), jnp.concatenate([pair, swapped], axis=0)


def collect(mine_of, other_of, tag):
    got = core_pair(half(other_of(0, None)))
    rows = got.shape[0] // 4
    if int(tag) in OUT_DIRECT:
        cut = 3 * rows
        if int(tag) in SPLIT:
            near = half(mine_of(rows, cut) + f32(got[rows:cut]))
            last = half(mine_of(cut, None) + f32(got[cut:]))
            own = mine_of(0, rows) + f32(got[:rows])
        else:
            part = half(mine_of(0, None) + f32(got))
            own, near, last = part[:rows], part[rows:cut], part[cut:]
        far = corner(last)
        side = first_side(near)
        swapped = core_pair(side[rows:])
        return f32(own) + f32(far) + f32(side[:rows]) + f32(swapped)
    part = half(mine_of(0, None) + f32(got))
    own = part[:rows]
    far = second_side(part[3 * rows :])
    near = half(f32(part[rows : 2 * rows]) + f32(far))
    side = first_side(jnp.concatenate([near, part[2 * rows : 3 * rows]], axis=0))
    swapped = core_pair(side[rows:])
    return f32(own) + f32(side[:rows]) + f32(swapped)


def gather_plan(tokens, expert_ids, gate_weights, w_gate, w_up, w_down):
    experts, shards = lax.axis_size("expert"), lax.axis_size("tensor")
    me, mz = lax.axis_index("expert"), lax.axis_index("tensor")
    cols = tokens.shape[1]
    units = w_gate.shape[2]
    hits = expert_ids[:, :, None] == jnp.arange(experts, dtype=jnp.int32)
    table = jnp.sum(jnp.where(hits, gate_weights[:, :, None], 0.0), axis=1)
    terms, rest = [], table
    for _ in range(3):
        term = lax.reduce_precision(rest, 8, 7)
        terms.append(half(term))
        rest = rest - term
    terms = jnp.concatenate(terms, axis=1)
    terms = jnp.pad(terms, ((0, 0), (0, 128 - terms.shape[1])))

    places = mz ^ jnp.arange(shards, dtype=jnp.int32)
    pairs = load_slices(places, [w_gate, w_up], 1, 2 << 20)
    downs = load_slices(places, [w_down], 2, 2 << 20)
    zs = {k: along(tokens, k) for k in range(1, shards)}
    acc = [0.0, 0.0]
    weight = None
    for n, ks in enumerate(IN_CHUNKS):
        parts = [tokens if k == 0 else zs[k] for k in ks]
        if n == TERMS_IN:
            parts.append(terms)
        both = spread(jnp.concatenate(parts, axis=1) if len(parts) > 1 else parts[0], str(n))
        for i, k in enumerate(ks):
            for h in range(2):
                acc[h] = acc[h] + jnp.dot(
                    both[h][:, i * cols : (i + 1) * cols],
                    pairs[k],
                    preferred_element_type=jnp.float32,
                )
        acc = list(lax.optimization_barrier(tuple(acc)))
        if n == TERMS_IN:
            pick = jnp.arange(3 * experts, dtype=jnp.int32) % experts == me
            weight = [
                jnp.sum(jnp.where(pick, f32(b[:, len(ks) * cols :][:, : 3 * experts]), 0.0), axis=1)
                for b in both
            ]
    hidden = [
        half(jax.nn.silu(a[:, :units]) * a[:, units:] * w[:, None]) for a, w in zip(acc, weight)
    ]
    sums, passed = {}, {}
    for n, ks in enumerate(OUT_CHUNKS):
        def product(h, start, stop):
            return jnp.concatenate(
                [jnp.dot(hidden[h][start:stop], downs[k], preferred_element_type=jnp.float32)
                    for k in ks
                ],
                axis=1,
            )

        total = collect(lambda *rows: product(0, *rows), lambda *rows: product(1, *rows), str(n))
        for i, k in enumerate(ks):
            sums[k] = total[:, i * cols : (i + 1) * cols]
            if k ^ 2 in passed:
                sums[k] = sums[k] + f32(passed[k ^ 2])
            if k:
                sums[k] = half(sums[k])
            if k > 2:
                passed[k] = along(sums[k], 2)
    mixed = sums[0]
    for k in range(1, shards):
        if k not in passed:
            mixed = mixed + f32(along(sums[k], k))
    return half(mixed)


def local(*args):
    tok_rows, top_count = args[1].shape
    experts, shards = lax.axis_size("expert"), lax.axis_size("tensor")
    capacity = min(tok_rows, 3 * tok_rows * top_count // (2 * experts))
    if capacity == tok_rows and experts == 1 << 3 and shards & (shards - 1) == 0 and shards > 2:
        return gather_plan(*args)
    return slot_plan(*args)


def solution(mesh):
    placed = (
        P("expert", "tensor"),
        P("expert", None),
        P("expert", None),
        P("expert", None, "tensor"),
        P("expert", None, "tensor"),
        P("expert", "tensor", None),
    )
    return jax.shard_map(
        local, mesh=mesh, in_specs=placed, out_specs=P("expert", "tensor"), check_vma=False
    )
```

```python
import jax
import jax.numpy as jnp
from jax import lax
from jax.experimental import pallas as pl
from jax.experimental.pallas import tpu as pltpu
from jax.sharding import PartitionSpec as P


IN_CHUNKS = [[0], [2], [1], [3]]
OUT_CHUNKS = [[3], [2], [1], [0]]
TERMS_IN = 1
LEND_IN = 1
LEND_OUT = 1
SPLIT = (1, 3)
IN_DIRECT = (0, 1, 3)
OUT_DIRECT = (0, 1, 2, 3)


def slot_plan(tokens, expert_ids, gate_weights, w_gate, w_up, w_down):
    experts = lax.axis_size("expert")
    tok_rows, top_count = expert_ids.shape
    capacity = min(tok_rows, 3 * tok_rows * top_count // (2 * experts))
    slots_all = experts * capacity
    flat_ids = expert_ids.reshape(-1)
    onehot = (flat_ids[:, None] == jnp.arange(experts, dtype=jnp.int32)[None, :]).astype(jnp.int32)
    slot_rank = jnp.sum((jnp.cumsum(onehot, axis=0) - onehot) * onehot, axis=1)
    places = (flat_ids * capacity + slot_rank).reshape(tok_rows, top_count)
    slot_range = jnp.arange(slots_all, dtype=jnp.int32)[None, :]
    selector = jnp.zeros((tok_rows, slots_all), jnp.float32)
    combine_weights = jnp.zeros((tok_rows, slots_all), jnp.float32)
    for choice_index in range(top_count):
        hit = places[:, choice_index][:, None] == slot_range
        selector = selector + hit.astype(jnp.float32)
        combine_weights = combine_weights + jnp.where(
            hit, gate_weights[:, choice_index][:, None], 0.0
        )
    selector = selector.astype(jnp.bfloat16)
    outgoing = lax.dot_general(
        selector, tokens, (((0,), (0,)), ((), ())), preferred_element_type=jnp.float32
    ).astype(jnp.bfloat16)
    arrived = lax.all_to_all(outgoing, "expert", split_axis=0, concat_axis=0, tiled=True)
    hidden_units = w_gate.shape[2]
    paired = jnp.concatenate([w_gate[0], w_up[0]], axis=1)
    gate_up = jnp.dot(
        lax.all_gather(arrived, "tensor", axis=1, tiled=True),
        paired,
        preferred_element_type=jnp.float32,
    )
    hidden = (jax.nn.silu(gate_up[:, :hidden_units]) * gate_up[:, hidden_units:]).astype(
        jnp.bfloat16
    )
    summed = lax.psum_scatter(
        lax.dot_general(
            w_down[0], hidden, (((0,), (1,)), ((), ())), preferred_element_type=jnp.float32
        ).astype(jnp.bfloat16),
        "tensor",
        scatter_dimension=0,
        tiled=True,
    )
    returned = lax.all_to_all(summed, "expert", split_axis=1, concat_axis=1, tiled=True)
    mixed = lax.dot_general(
        combine_weights,
        returned.astype(jnp.float32),
        (((1,), (1,)), ((), ())),
        precision=lax.Precision.HIGHEST,
        preferred_element_type=jnp.float32,
    )
    return mixed.astype(jnp.bfloat16)


def toward(a, move):
    experts, shards = lax.axis_size("expert"), lax.axis_size("tensor")
    pairs = []
    for e in range(experts):
        for z in range(shards):
            to_e, to_z = move(e, z)
            pairs.append((e * shards + z, to_e * shards + to_z))
    return lax.ppermute(a, ("expert", "tensor"), pairs)


def core_pair(a):
    return toward(a, lambda e, z: (e ^ 1, z))


def first_side(a):
    return toward(a, lambda e, z: (e ^ (2 << (e & 1)), z))


def second_side(a):
    return toward(a, lambda e, z: (e ^ (4 >> (e & 1)), z))


def corner(a):
    return toward(a, lambda e, z: (e ^ 6, z))


def along(a, k):
    return toward(a, lambda e, z: (e, z ^ k))


def f32(a):
    return a.astype(jnp.float32)


def half(a):
    return a.astype(jnp.bfloat16)


def load_slices(places, sources, dim, grant):
    shard = sources[0].shape[dim] // lax.axis_size("tensor")
    shape = list(sources[0].shape[1:])
    shape[dim - 1] = shard
    width, count = shape[1], places.shape[0]

    def kernel(places_ref, *refs):
        ins, outs, sem = refs[: len(sources)], refs[len(sources) : -1], refs[-1]
        copies = []
        for k in range(count):
            part = pl.ds(pl.multiple_of(places_ref[k] * shard, shard), shard)
            for n, ref in enumerate(ins):
                src = ref.at[0, part, :] if dim == 1 else ref.at[0, :, part]
                dst = outs[k].at[:, pl.ds(n * width, width)]
                copies.append(pltpu.make_async_copy(src, dst, sem.at[len(copies)]))
        for copy in copies:
            copy.start()
        for copy in copies:
            copy.wait()

    out = pltpu.VMEM((shape[0], width * len(sources)), sources[0].dtype)
    return pl.pallas_call(
        kernel,
        out_shape=[out] * count,
        in_specs=[pl.BlockSpec(memory_space=pltpu.SMEM)]
        + [pl.BlockSpec(memory_space=pl.ANY)] * len(sources),
        out_specs=[pl.BlockSpec(memory_space=pltpu.VMEM)] * count,
        scratch_shapes=[pltpu.SemaphoreType.DMA((count * len(sources),))],
        compiler_params=pltpu.CompilerParams(vmem_limit_bytes=grant),
    )(places, *[pltpu.with_memory_space_constraint(a, pltpu.HBM) for a in sources])


def spread(a, tag):
    rows = a.shape[0]
    pair = core_pair(a)
    side = first_side(jnp.concatenate([a, pair], axis=0))
    far = corner(a) if int(tag) in IN_DIRECT else second_side(side[:rows])
    brought = jnp.concatenate([side, far], axis=0)
    swapped = core_pair(brought)
    return jnp.concatenate([a, brought], axis=0), jnp.concatenate([pair, swapped], axis=0)


def collect(mine_of, other_of, tag):
    got = core_pair(half(other_of(0, None)))
    rows = got.shape[0] // 4
    if int(tag) in OUT_DIRECT:
        cut = 3 * rows
        if int(tag) in SPLIT:
            near = half(mine_of(rows, cut) + f32(got[rows:cut]))
            last = half(mine_of(cut, None) + f32(got[cut:]))
            own = mine_of(0, rows) + f32(got[:rows])
        else:
            part = half(mine_of(0, None) + f32(got))
            own, near, last = part[:rows], part[rows:cut], part[cut:]
        far = corner(last)
        side = first_side(near)
        swapped = core_pair(side[rows:])
        return f32(own) + f32(far) + f32(side[:rows]) + f32(swapped)
    part = half(mine_of(0, None) + f32(got))
    own = part[:rows]
    far = second_side(part[3 * rows :])
    near = half(f32(part[rows : 2 * rows]) + f32(far))
    side = first_side(jnp.concatenate([near, part[2 * rows : 3 * rows]], axis=0))
    swapped = core_pair(side[rows:])
    return f32(own) + f32(side[:rows]) + f32(swapped)


def gather_plan(tokens, expert_ids, gate_weights, w_gate, w_up, w_down):
    experts, shards = lax.axis_size("expert"), lax.axis_size("tensor")
    me, mz = lax.axis_index("expert"), lax.axis_index("tensor")
    cols = tokens.shape[1]
    units = w_gate.shape[2]
    hits = expert_ids[:, :, None] == jnp.arange(experts, dtype=jnp.int32)
    table = jnp.sum(jnp.where(hits, gate_weights[:, :, None], 0.0), axis=1)
    terms, rest = [], table
    for _ in range(3):
        term = lax.reduce_precision(rest, 8, 7)
        terms.append(half(term))
        rest = rest - term
    terms = jnp.concatenate(terms, axis=1)
    terms = jnp.pad(terms, ((0, 0), (0, 128 - terms.shape[1])))

    places = mz ^ jnp.arange(shards, dtype=jnp.int32)
    pairs = load_slices(places, [w_gate, w_up], 1, 2 << 20)
    downs = load_slices(places, [w_down], 2, 2 << 20)
    zs = {k: along(tokens, k) for k in range(1 + LEND_IN, shards)}
    acc = [0.0, 0.0]
    weight = None
    for n, ks in enumerate(IN_CHUNKS):
        parts = [tokens if k == 0 else zs.get(k) for k in ks]
        if n == TERMS_IN:
            parts.append(terms)
        if ks == [1] and LEND_IN:
            mine = along(first, 1)
            both = mine, core_pair(mine)
        else:
            both = spread(
                jnp.concatenate(parts, axis=1) if len(parts) > 1 else parts[0], str(n)
            )
        if n == 0:
            first = both[0]
        for i, k in enumerate(ks):
            for h in range(2):
                acc[h] = acc[h] + jnp.dot(
                    both[h][:, i * cols : (i + 1) * cols],
                    pairs[k],
                    preferred_element_type=jnp.float32,
                )
        acc = list(lax.optimization_barrier(tuple(acc)))
        if n == TERMS_IN:
            pick = jnp.arange(3 * experts, dtype=jnp.int32) % experts == me
            weight = [
                jnp.sum(jnp.where(pick, f32(b[:, len(ks) * cols :][:, : 3 * experts]), 0.0), axis=1)
                for b in both
            ]
    hidden = [
        half(jax.nn.silu(a[:, :units]) * a[:, units:] * w[:, None]) for a, w in zip(acc, weight)
    ]
    sums, lent = {}, []
    for n, ks in enumerate(OUT_CHUNKS):
        def product(h, start, stop):
            return jnp.concatenate(
                [jnp.dot(hidden[h][start:stop], downs[k], preferred_element_type=jnp.float32)
                    for k in ks
                ],
                axis=1,
            )

        if ks == [1] and LEND_OUT:
            got = core_pair(half(product(1, 0, None)))
            part = half(product(0, 0, None) + f32(got))
            lent.append(along(part, 1))
            continue
        total = collect(lambda *rows: product(0, *rows) + sum(f32(v[slice(*rows)]) for v in lent if ks == [0]), lambda *rows: product(1, *rows), str(n))
        for i, k in enumerate(ks):
            sums[k] = total[:, i * cols : (i + 1) * cols]
            if k:
                sums[k] = half(sums[k])
    mixed = sums[0]
    for k in range(1, shards):
        if k in sums:
            mixed = mixed + f32(along(sums[k], k))
    return half(mixed)


def local(*args):
    tok_rows, top_count = args[1].shape
    experts, shards = lax.axis_size("expert"), lax.axis_size("tensor")
    capacity = min(tok_rows, 3 * tok_rows * top_count // (2 * experts))
    if capacity == tok_rows and experts == 1 << 3 and shards == len(IN_CHUNKS):
        return gather_plan(*args)
    return slot_plan(*args)


def solution(mesh):
    placed = (
        P("expert", "tensor"),
        P("expert", None),
        P("expert", None),
        P("expert", None, "tensor"),
        P("expert", None, "tensor"),
        P("expert", "tensor", None),
    )
    return jax.shard_map(
        local, mesh=mesh, in_specs=placed, out_specs=P("expert", "tensor"), check_vma=False
    )
```
